32 devices in a mesh: dp: 4 (over z), shard: 8 (over y, x, core).
Axes of the slice: x: 2, y: 2, z: 4, core: 2. Of those that a mesh axis runs over, the one named last changes fastest.
Arguments:
- hidden: bfloat16 [192, 256, 1024], P(('dp', 'shard')), may hold values from -40 to 40, as said below
- lengths: int32 [192], replicated, may hold values from 16 to 256
- dealing: int32 [192], replicated, may hold values from 0 to 191, each once
- candidates: int32 [192, 64], P(('dp', 'shard')), may hold values from 0 to 131071
- index_rows: bfloat16 [131072, 1024], P(('dp', 'shard')), may hold values from -6 to 6
- qkv_weight: bfloat16 [1024, 3072], replicated, may hold values from -0.1875 to 0.1875
- qkv_bias: float32 [3072], replicated, may hold values from -3 to 3
- out_weight: bfloat16 [1024, 1024], replicated, may hold values from -0.1875 to 0.1875
- out_bias: float32 [1024], replicated, may hold values from -3 to 3
- norm_gain: float32 [1024], replicated, may hold values from 0.25 to 1.75
- norm_shift: float32 [1024], replicated, may hold values from -3 to 3
Outputs:
- scores: float32 [192, 64], P(('dp', 'shard'))
The draws below stay inside these ranges and needn't reach their ends.
Inputs may be any that keep to these rules, and one draw needn't show every extreme that they name: dealing names every text once. `hidden`: token states of order one, some much larger.
All inputs are finite; a program needn't handle non-finite values.
Results may differ from the reference program's by a relative error of at most 0.0044.
Values may be sent and summed in bfloat16 or wider, within the bound.
A program may use at most 128 MiB of HBM per device.

```python
import jax
import jax.numpy as jnp
from jax import lax

D = 1024
HEADS = 16
HEAD = 64
LMAX = 256
K = 64
TEXTS = 192
ROWS = 131072


def draw_hidden(key, part):
    shape = (TEXTS, LMAX, D)
    values = jnp.clip(jax.random.normal(key, shape, jnp.float32), -6.0, 6.0)
    return values.astype(jnp.bfloat16)


def with_ends(array, stream_key, smallest, top_value):
    place = [jax.random.randint(jax.random.fold_in(stream_key, axis), (), 0, length) for axis, length in enumerate(array.shape)]
    widest = array.shape.index(max(array.shape))
    next_to = place[:widest] + [(place[widest] + 1) % array.shape[widest]] + place[widest + 1:]
    return array.at[tuple(place)].set(smallest).at[tuple(next_to)].set(top_value)


def level_of(key, dims, cuts, low, top_value):
    loudness = 1.0
    for dim, blocks in cuts:
        heights = jax.random.uniform(jax.random.fold_in(jax.random.fold_in(key, 6), dim), (blocks,), jnp.float32, low / len(cuts), top_value / len(cuts))
        loudness = loudness * jnp.repeat(jnp.exp(heights), dims[dim] // blocks).reshape((-1,) + (1,) * (len(dims) - 1 - dim))
    return loudness


def bell_draw(stream_key, dims, width, most, shards=(), kind=jnp.bfloat16):
    entries = width * jax.random.normal(stream_key, dims, jnp.float32)
    if shards:
        entries = entries * level_of(stream_key, dims, shards, -0.22, 0.18)
    return jnp.clip(entries, -most, most).astype(kind)


def setup_inputs(seed: int = 0) -> dict:
    seeds = jax.random.split(jax.random.key(seed), 12)
    return {
        "hidden": draw_hidden(jax.random.fold_in(seeds[11], 71), 0),
        "lengths": with_ends(jax.random.randint(seeds[1], (TEXTS,), LMAX // 16, LMAX + 1), jax.random.fold_in(seeds[1], 1), LMAX // 16, LMAX).astype(jnp.int32),
        "dealing": jax.random.permutation(seeds[2], TEXTS).astype(jnp.int32),
        "candidates": with_ends(jax.random.randint(seeds[3], (TEXTS, K), 0, ROWS), jax.random.fold_in(seeds[3], 1), 0, ROWS - 1).astype(jnp.int32),
        "index_rows": bell_draw(seeds[4], (ROWS, D), 1.0, 6.0, ((0, 32),)),
        "qkv_weight": bell_draw(seeds[5], (D, 3 * D), D ** -0.5, 0.1875),
        "qkv_bias": bell_draw(seeds[6], (3 * D,), 0.5, 3.0, (), jnp.float32),
        "out_weight": bell_draw(seeds[7], (D, D), D ** -0.5, 0.1875),
        "out_bias": bell_draw(seeds[8], (D,), 0.5, 3.0, (), jnp.float32),
        "norm_gain": jnp.clip(1.0 + 0.15 * jax.random.normal(seeds[9], (D,), jnp.float32), 0.25, 1.75),
        "norm_shift": bell_draw(seeds[10], (D,), 0.5, 3.0, (), jnp.float32),
    }


def encode_text(states, text_len, qkv_weight, qkv_bias, out_weight, out_bias, norm_gain, norm_shift):
    model_width = states.shape[1]
    seq_len = states.shape[0]
    qkv = (jnp.dot(states, qkv_weight, preferred_element_type=jnp.float32) + qkv_bias).astype(jnp.bfloat16)
    q_part = qkv[:, :model_width].reshape(seq_len, HEADS, HEAD).astype(jnp.float32)
    k_part = qkv[:, model_width:2 * model_width].reshape(seq_len, HEADS, HEAD).astype(jnp.float32)
    v_part = qkv[:, 2 * model_width:].reshape(seq_len, HEADS, HEAD).astype(jnp.float32)
    logits = jnp.einsum('qhd,khd->hqk', q_part, k_part) * (1.0 / HEAD ** 0.5)
    positions = jnp.arange(seq_len, dtype=jnp.int32)
    key_valid = positions < text_len
    logits = jnp.where(key_valid[None, None, :], logits, -1e+30)
    peak = lax.optimization_barrier(jnp.max(logits, axis=-1, keepdims=True))
    weights = jnp.exp(logits - peak)
    probs = (weights / lax.optimization_barrier(jnp.sum(weights, axis=-1, keepdims=True))).astype(jnp.bfloat16)
    context = jnp.einsum('hqk,khd->qhd', probs.astype(jnp.float32), v_part)
    context = context.reshape(seq_len, model_width).astype(jnp.bfloat16)
    resid = states.astype(jnp.float32) + jnp.dot(context, out_weight, preferred_element_type=jnp.float32) + out_bias
    centre = lax.optimization_barrier(jnp.mean(resid, axis=-1, keepdims=True))
    spread = lax.optimization_barrier(jnp.mean((resid - centre) ** 2, axis=-1, keepdims=True))
    normed = (resid - centre) * lax.rsqrt(spread + 1e-05) * norm_gain + norm_shift
    pooled = lax.optimization_barrier(jnp.sum(jnp.where(key_valid[:, None], normed, 0.0), axis=0)) / text_len.astype(jnp.float32)
    queries = pooled * lax.rsqrt(jnp.sum(pooled * pooled) + 1e-06)
    return queries.astype(jnp.bfloat16)

def reference(hidden, lengths, dealing, candidates, index_rows, qkv_weight, qkv_bias, out_weight, out_bias, norm_gain, norm_shift):
    slot_lens = lengths[dealing]

    def one_slot(pair):
        return encode_text(pair[0], pair[1], qkv_weight, qkv_bias, out_weight, out_bias, norm_gain, norm_shift)
    slot_queries = lax.map(one_slot, (hidden, slot_lens))
    text_queries = jnp.zeros_like(slot_queries).at[dealing].set(slot_queries)

    def one_text(pair):
        fetched = index_rows[pair[1]]
        return jnp.dot(fetched, pair[0], preferred_element_type=jnp.float32)
    return lax.map(one_text, (text_queries, candidates))
```

```python
import functools

import jax
import jax.numpy as jnp
from jax import lax
from jax.experimental import pallas as pl
from jax.experimental.pallas import tpu as pltpu
from jax.sharding import PartitionSpec as P

HEADS = 16
HEAD = 64
AXES = ("dp", "shard")
LANES = 128


def my_rank():
    return lax.axis_index("dp") * lax.axis_size("shard") + lax.axis_index("shard")


def coords(rank):
    shard_count = lax.axis_size("shard")
    return (rank // shard_count, rank % shard_count)


def encode_kernel(
    text_dev,
    lengths_ref,
    dealing_ref,
    hidden_ref,
    qkv_weight_ref,
    qkv_bias_ref,
    out_weight_ref,
    out_bias_ref,
    gain_ref,
    shift_ref,
    query_ref,
    qkv_ref,
    context_ref,
    rows_ref,
):
    step = pl.program_id(0)
    text_len = lengths_ref[dealing_ref[my_rank() * text_dev + step]]
    seq_len, width = hidden_ref.shape[1], hidden_ref.shape[2]
    states = hidden_ref[0]

    chunk = 512
    for start in range(0, 3 * width, chunk):
        cols = slice(start, start + chunk)
        part = (
            jnp.dot(states, qkv_weight_ref[:, cols], preferred_element_type=jnp.float32)
            + qkv_bias_ref[:, cols]
        )
        if start < width:
            part = part * (1.0 / HEAD**0.5)
        qkv_ref[:, cols] = part.astype(jnp.bfloat16)

    lane = lax.broadcasted_iota(jnp.int32, (seq_len, LANES), 1)
    first = lane < HEAD
    key_pos = lax.broadcasted_iota(jnp.int32, (1, seq_len), 1)
    key_bias = jnp.where(key_pos < text_len, 0.0, -1e30).astype(jnp.float32)
    zero = jnp.zeros((seq_len, LANES), jnp.bfloat16)
    ones = jnp.ones((seq_len, LANES), jnp.bfloat16)
    ones_a = jnp.where(first, ones, zero)
    ones_b = jnp.where(first, zero, ones)
    for pair in range(width // LANES):
        base = pair * LANES
        q2 = qkv_ref[:, base : base + LANES]
        k2 = qkv_ref[:, width + base : width + base + LANES]
        v2 = qkv_ref[:, 2 * width + base : 2 * width + base + LANES]
        probs = []
        for keys in (jnp.where(first, k2, zero), jnp.where(first, zero, k2)):
            logits = lax.dot_general(
                q2, keys, (((1,), (1,)), ((), ())), preferred_element_type=jnp.float32
            )
            logits = logits + key_bias
            peak = jnp.max(logits, axis=-1, keepdims=True)
            probs.append(jnp.exp(logits - peak).astype(jnp.bfloat16))
        both = jnp.concatenate(probs, axis=1)
        values = jnp.concatenate(
            [
                jnp.concatenate([jnp.where(first, v2, zero), ones_a], axis=1),
                jnp.concatenate([jnp.where(first, zero, v2), ones_b], axis=1),
            ],
            axis=0,
        )
        mixed = jnp.dot(both, values, preferred_element_type=jnp.float32)
        context_ref[:, base : base + LANES] = (mixed[:, :LANES] / mixed[:, LANES:]).astype(
            jnp.bfloat16
        )

    resid = (
        states.astype(jnp.float32)
        + jnp.dot(context_ref[...], out_weight_ref[...], preferred_element_type=jnp.float32)
        + out_bias_ref[...]
    )
    centre = jnp.mean(resid, axis=-1, keepdims=True)
    resid = resid - centre
    spread = jnp.mean(resid * resid, axis=-1, keepdims=True)
    row_pos = lax.broadcasted_iota(jnp.int32, (seq_len, 1), 0)
    scale = jnp.where(row_pos < text_len, lax.rsqrt(spread + 1e-05), 0.0)
    total = jnp.sum(resid * scale, axis=0, keepdims=True)
    pooled = total / text_len.astype(jnp.float32) * gain_ref[...] + shift_ref[...]
    query = pooled * lax.rsqrt(jnp.sum(pooled * pooled, axis=-1, keepdims=True) + 1e-06)

    @pl.when(step == 0)
    def _():
        rows_ref[...] = jnp.zeros_like(rows_ref)

    rows_ref[pl.ds(step, 1), :] = query

    @pl.when(step == text_dev - 1)
    def _():
        query_ref[...] = rows_ref[...].astype(jnp.bfloat16)


def greet(device_count, me):
    barrier = pltpu.get_barrier_semaphore()

    def signal(off, carry):
        pl.semaphore_signal(
            barrier,
            inc=1,
            device_id=coords(lax.rem(me + off, device_count)),
            device_id_type=pl.DeviceIdType.MESH,
        )
        return carry

    lax.fori_loop(1, device_count, signal, 0)
    pl.semaphore_wait(barrier, device_count - 1)


def gather_kernel(
    device_count, query_ref, cand_ref, queries_ref, cands_ref, send_sems, recv_sems, local_sems
):
    me = my_rank()
    greet(device_count, me)
    pairs = ((query_ref, queries_ref), (cand_ref, cands_ref))

    def remote(which, peer, source):
        src, dst = pairs[which]
        return pltpu.make_async_remote_copy(
            src_ref=src,
            dst_ref=dst.at[source],
            send_sem=send_sems.at[which, peer],
            recv_sem=recv_sems.at[which, source],
            device_id=coords(peer),
            device_id_type=pl.DeviceIdType.MESH,
        )

    def send(off, carry):
        peer = lax.rem(me + off, device_count)
        for which in range(2):
            remote(which, peer, me).start()
        return carry

    lax.fori_loop(1, device_count, send, 0)
    local = [
        pltpu.make_async_copy(src, dst.at[me], local_sems.at[which])
        for which, (src, dst) in enumerate(pairs)
    ]
    for copy in local:
        copy.start()
    for copy in local:
        copy.wait()

    def finish(off, carry):
        peer = lax.rem(me + off, device_count)
        for which in range(2):
            remote(which, peer, peer).wait_recv()
            remote(which, peer, me).wait_send()
        return carry

    lax.fori_loop(1, device_count, finish, 0)


def score_kernel(
    dealt_ref, query_ref, cand_ref, index_ref, out_ref, text_query_ref, text_dev
):
    step = pl.program_id(0)
    padded = query_ref.shape[0]
    rows_step = index_ref.shape[0]

    @pl.when(step == 0)
    def _():
        spot = lax.broadcasted_iota(jnp.int32, (padded, padded), 0)
        pick = jnp.where(dealt_ref[...] == spot, 1.0, 0.0).astype(jnp.bfloat16)
        text_query_ref[...] = jnp.dot(
            pick, query_ref[...], preferred_element_type=jnp.float32
        ).astype(jnp.bfloat16)
        out_ref[...] = jnp.zeros_like(out_ref)

    scores = lax.dot_general(
        text_query_ref[...],
        index_ref[...],
        (((1,), (1,)), ((), ())),
        preferred_element_type=jnp.float32,
    )
    local = cand_ref[...] - (my_rank() * pl.num_programs(0) + step) * rows_step
    group = local >> 7
    lane = local & (LANES - 1)
    total = out_ref[...]
    for part in range(rows_step // LANES):
        found = jnp.take_along_axis(
            scores[:, part * LANES : (part + 1) * LANES], lane, axis=1, mode="promise_in_bounds"
        )
        total = jnp.where(group == part, found, total)
    out_ref[...] = total


def exchange_kernel(device_count, terms_ref, out_ref, arrived, send_sems, recv_sems):
    me = my_rank()
    greet(device_count, me)

    def remote(peer, source):
        return pltpu.make_async_remote_copy(
            src_ref=terms_ref.at[peer],
            dst_ref=arrived.at[source],
            send_sem=send_sems.at[peer],
            recv_sem=recv_sems.at[source],
            device_id=coords(peer),
            device_id_type=pl.DeviceIdType.MESH,
        )

    def send(off, carry):
        remote(lax.rem(me + off, device_count), me).start()
        return carry

    lax.fori_loop(1, device_count, send, 0)
    arrived[me] = terms_ref[me]

    def finish(off, carry):
        peer = lax.rem(me + off, device_count)
        remote(peer, peer).wait_recv()
        remote(peer, me).wait_send()
        return carry

    lax.fori_loop(1, device_count, finish, 0)
    total = jnp.sum(arrived[...], axis=0)
    out_ref[...] = total[: out_ref.shape[0], : out_ref.shape[1]]


def shards(
    hidden,
    lengths,
    dealing,
    candidates,
    index_rows,
    qkv_weight,
    qkv_bias,
    out_weight,
    out_bias,
    norm_gain,
    norm_shift,
):
    text_dev, seq_len, width = hidden.shape
    device_count = lax.axis_size(AXES)
    cand_count = candidates.shape[1]
    slots = -(-text_dev // 8) * 8
    padded = device_count * slots
    vmem = pl.BlockSpec(memory_space=pltpu.VMEM)

    def whole(*shape):
        return pl.BlockSpec(
            shape, lambda *_: (0,) * len(shape), pipeline_mode=pl.Buffered(1)
        )

    query = pl.pallas_call(
        functools.partial(encode_kernel, text_dev),
        grid_spec=pltpu.PrefetchScalarGridSpec(
            num_scalar_prefetch=2,
            grid=(text_dev,),
            in_specs=[
                pl.BlockSpec((1, seq_len, width), lambda i, *_: (i, 0, 0)),
                whole(width, 3 * width),
                whole(1, 3 * width),
                whole(width, width),
                whole(1, width),
                whole(1, width),
                whole(1, width),
            ],
            out_specs=pl.BlockSpec((slots, width), lambda i, *_: (0, 0)),
            scratch_shapes=[
                pltpu.VMEM((seq_len, 3 * width), jnp.bfloat16),
                pltpu.VMEM((seq_len, width), jnp.bfloat16),
                pltpu.VMEM((slots, width), jnp.float32),
            ],
        ),
        out_shape=jax.ShapeDtypeStruct((slots, width), jnp.bfloat16),
        compiler_params=pltpu.CompilerParams(vmem_limit_bytes=40 << 20),
        name="encode",
    )(
        lengths,
        dealing,
        hidden,
        qkv_weight,
        qkv_bias[None, :],
        out_weight,
        out_bias[None, :],
        norm_gain[None, :],
        norm_shift[None, :],
    )

    cand_block = jnp.pad(
        candidates, ((0, slots - text_dev), (0, LANES - cand_count)), constant_values=-1
    )
    queries, cands = pl.pallas_call(
        functools.partial(gather_kernel, device_count),
        in_specs=[vmem, vmem],
        out_specs=[vmem, vmem],
        out_shape=[
            jax.ShapeDtypeStruct((device_count, slots, width), jnp.bfloat16),
            jax.ShapeDtypeStruct((device_count, slots, LANES), jnp.int32),
        ],
        scratch_shapes=[
            pltpu.SemaphoreType.DMA((2, device_count)),
            pltpu.SemaphoreType.DMA((2, device_count)),
            pltpu.SemaphoreType.DMA((2,)),
        ],
        compiler_params=pltpu.CompilerParams(collective_id=0, has_side_effects=True),
        name="gather",
    )(query, cand_block)

    dealt = dealing.reshape(device_count, text_dev)
    dealt = dealt // text_dev * slots + dealt % text_dev
    dealt = jnp.pad(dealt, ((0, 0), (0, slots - text_dev)), constant_values=-1)
    rows_step = 1024
    terms = pl.pallas_call(
        functools.partial(score_kernel, text_dev=text_dev),
        grid=(index_rows.shape[0] // rows_step,),
        in_specs=[
            whole(1, padded),
            whole(padded, width),
            whole(padded, LANES),
            pl.BlockSpec((rows_step, width), lambda i: (i, 0)),
        ],
        out_specs=pl.BlockSpec((padded, LANES), lambda i: (0, 0)),
        out_shape=jax.ShapeDtypeStruct((padded, LANES), jnp.float32),
        scratch_shapes=[pltpu.VMEM((padded, width), jnp.bfloat16)],
        compiler_params=pltpu.CompilerParams(vmem_limit_bytes=40 << 20),
        name="score",
    )(
        dealt.reshape(1, padded),
        queries.reshape(padded, width),
        cands.reshape(padded, LANES),
        index_rows,
    )

    return pl.pallas_call(
        functools.partial(exchange_kernel, device_count),
        in_specs=[vmem],
        out_specs=vmem,
        out_shape=jax.ShapeDtypeStruct((text_dev, cand_count), jnp.float32),
        scratch_shapes=[
            pltpu.VMEM((device_count, slots, LANES), jnp.float32),
            pltpu.SemaphoreType.DMA((device_count,)),
            pltpu.SemaphoreType.DMA((device_count,)),
        ],
        compiler_params=pltpu.CompilerParams(collective_id=1, has_side_effects=True),
        name="exchange",
    )(terms.reshape(device_count, slots, LANES))


def solution(mesh):
    in_specs = (
        P(("dp", "shard"), None, None),
        P(),
        P(),
        P(("dp", "shard"), None),
        P(("dp", "shard"), None),
        P(),
        P(),
        P(),
        P(),
        P(),
        P(),
    )
    out_specs = P(("dp", "shard"), None)
    return jax.shard_map(shards, mesh=mesh, in_specs=in_specs, out_specs=out_specs, check_vma=False)
```

```python
import functools

import jax
import jax.numpy as jnp
from jax import lax
from jax.experimental import pallas as pl
from jax.experimental.pallas import tpu as pltpu
from jax.sharding import PartitionSpec as P

HEADS = 16
HEAD = 64
LANES = 128


SLOTS = 8
BATCH = 2


def encode_text(
    step, text_len, hidden_ref, weights, bias_ref, out_bias_ref, gain_ref, shift_ref, scratch
):
    qkv_weight, out_weight, qkv_wait, out_wait = weights
    qkv_ref, context_ref = scratch
    seq_len, width = hidden_ref.shape[1], hidden_ref.shape[2]
    states = hidden_ref[0]

    chunk = 512
    for start in range(0, 3 * width, chunk):
        if start % width == 0:
            pl.when(step == 0)(qkv_wait[start // width])
        cols = slice(start, start + chunk)
        part = (
            jnp.dot(states, qkv_weight[:, cols], preferred_element_type=jnp.float32)
            + bias_ref[:, cols]
        )
        if start < width:
            part = part * (1.0 / HEAD**0.5)
        qkv_ref[:, cols] = part.astype(jnp.bfloat16)

    lane = lax.broadcasted_iota(jnp.int32, (seq_len, LANES), 1)
    first = lane < HEAD
    key_pos = lax.broadcasted_iota(jnp.int32, (1, seq_len), 1)
    key_bias = jnp.where(key_pos < text_len, 0.0, -1e30).astype(jnp.float32)
    zero = jnp.zeros((seq_len, LANES), jnp.bfloat16)
    ones = jnp.ones((seq_len, LANES), jnp.bfloat16)
    ones_a = jnp.where(first, ones, zero)
    ones_b = jnp.where(first, zero, ones)
    for pair in range(width // LANES):
        base = pair * LANES
        q2 = qkv_ref[:, base : base + LANES]
        k2 = qkv_ref[:, width + base : width + base + LANES]
        v2 = qkv_ref[:, 2 * width + base : 2 * width + base + LANES]
        probs = []
        for keys in (jnp.where(first, k2, zero), jnp.where(first, zero, k2)):
            logits = lax.dot_general(
                q2, keys, (((1,), (1,)), ((), ())), preferred_element_type=jnp.float32
            )
            logits = logits + key_bias
            peak = jnp.max(logits, axis=-1, keepdims=True)
            probs.append(jnp.exp(logits - peak).astype(jnp.bfloat16))
        both = jnp.concatenate(probs, axis=1)
        values = jnp.concatenate(
            [
                jnp.concatenate([jnp.where(first, v2, zero), ones_a], axis=1),
                jnp.concatenate([jnp.where(first, zero, v2), ones_b], axis=1),
            ],
            axis=0,
        )
        mixed = jnp.dot(both, values, preferred_element_type=jnp.float32)
        context_ref[:, base : base + LANES] = (mixed[:, :LANES] / mixed[:, LANES:]).astype(
            jnp.bfloat16
        )

    pl.when(step == 0)(out_wait)
    resid = (
        states.astype(jnp.float32)
        + jnp.dot(context_ref[...], out_weight[...], preferred_element_type=jnp.float32)
        + out_bias_ref[...]
    )
    centre = jnp.mean(resid, axis=-1, keepdims=True)
    resid = resid - centre
    spread = jnp.mean(resid * resid, axis=-1, keepdims=True)
    row_pos = lax.broadcasted_iota(jnp.int32, (seq_len, 1), 0)
    scale = jnp.where(row_pos < text_len, lax.rsqrt(spread + 1e-05), 0.0)
    total = jnp.sum(resid * scale, axis=0, keepdims=True)
    pooled = total / text_len.astype(jnp.float32) * gain_ref[...] + shift_ref[...]
    return pooled * lax.rsqrt(jnp.sum(pooled * pooled, axis=-1, keepdims=True) + 1e-06)


def slot_order(entries, rows, dp_count, shard_count, text_dev):
    block, row = entries // rows, entries % rows
    place = ((block % dp_count) * shard_count + block // dp_count) * text_dev + row
    return jnp.where(row < text_dev, place, -1)


def program_kernel(
    dp_count,
    shard_count,
    text_dev,
    lengths_ref,
    dealing_ref,
    hidden_ref,
    dealt_ref,
    cand_ref,
    qkv_bias_ref,
    out_bias_ref,
    gain_ref,
    shift_ref,
    qkv_weight_hbm,
    out_weight_hbm,
    index_hbm,
    out_ref,
    qkv_weight,
    out_weight,
    index_rows,
    qkv_ref,
    context_ref,
    fold_ref,
    queries,
    cands,
    wide_queries,
    slot_queries,
    text_queries,
    pick_ref,
    terms,
    arrived,
    sums,
    arrived_dp,
    load_sems,
    dp_send,
    dp_recv,
    shard_send,
    shard_recv,
):
    step = pl.program_id(0)
    my_dp, my_shard = lax.axis_index("dp"), lax.axis_index("shard")
    me = my_dp * shard_count + my_shard
    width = hidden_ref.shape[2]
    pieces = width // LANES
    padded = dp_count * shard_count * SLOTS
    compact = dp_count * shard_count * text_dev

    def dp_peer(off):
        return lax.rem(my_dp + off, dp_count)

    def shard_peer(off):
        return lax.rem(my_shard + off, shard_count)

    def to_dp(src, dst, which, off):
        return pltpu.make_async_remote_copy(
            src_ref=src,
            dst_ref=dst,
            send_sem=dp_send.at[which, off],
            recv_sem=dp_recv.at[which, off],
            device_id=(dp_peer(off), my_shard),
            device_id_type=pl.DeviceIdType.MESH,
        )

    def to_shard(src, dst, which, off):
        return pltpu.make_async_remote_copy(
            src_ref=src,
            dst_ref=dst,
            send_sem=shard_send.at[which, off],
            recv_sem=shard_recv.at[which, off],
            device_id=(my_dp, shard_peer(off)),
            device_id_type=pl.DeviceIdType.MESH,
        )

    tail = max(text_dev - BATCH, 1)
    spans = [pl.ds(0, tail), pl.ds(tail, text_dev - tail)]

    def own(which, dp, shard):
        if which == 2:
            return cands.at[shard, dp]
        return queries.at[shard, dp, spans[which]]

    def column(which, shard):
        if which == 2:
            return cands.at[shard]
        return queries.at[shard, :, spans[which]]

    def dp_start(which):
        for off in range(1, dp_count):
            block = own(which, my_dp, my_shard)
            to_dp(block, block, which, off).start()

    def dp_finish(which):
        for off in range(1, dp_count):
            block = own(which, lax.rem(my_dp + dp_count - off, dp_count), my_shard)
            to_dp(block, block, which, off).wait_recv()
            to_dp(block, block, which, off).wait_send()

    def shard_start(which):
        for off in range(1, shard_count):
            block = column(which, my_shard)
            to_shard(block, block, which, off).start()

    def shard_finish(which):
        for off in range(1, shard_count):
            block = column(which, lax.rem(my_shard + shard_count - off, shard_count))
            to_shard(block, block, which, off).wait_recv()
            to_shard(block, block, which, off).wait_send()

    loads = [
        pltpu.make_async_copy(
            qkv_weight_hbm.at[:, pl.ds(part * width, width)],
            qkv_weight.at[:, pl.ds(part * width, width)],
            load_sems.at[part],
        )
        for part in range(3)
    ]
    loads.append(pltpu.make_async_copy(out_weight_hbm, out_weight, load_sems.at[3]))
    loads.append(pltpu.make_async_copy(index_hbm, index_rows, load_sems.at[4]))
    barrier = pltpu.get_barrier_semaphore()

    @pl.when(step == 0)
    def _():
        for load in loads:
            load.start()
        for off in range(1, dp_count):
            pl.semaphore_signal(
                barrier,
                inc=1,
                device_id=(dp_peer(off), my_shard),
                device_id_type=pl.DeviceIdType.MESH,
            )
        for off in range(1, shard_count):
            pl.semaphore_signal(
                barrier,
                inc=1,
                device_id=(my_dp, shard_peer(off)),
                device_id_type=pl.DeviceIdType.MESH,
            )
        mine = cands.at[my_shard, my_dp]
        mine[...] = jnp.full((SLOTS, LANES), -1, jnp.int32)
        mine[:text_dev, : cand_ref.shape[1]] = cand_ref[...]
        texts = slot_order(
            lax.broadcasted_iota(jnp.int32, (padded, 1), 0), SLOTS, dp_count, shard_count, text_dev
        )
        slots = slot_order(
            lax.broadcasted_iota(jnp.int32, (1, compact), 1),
            text_dev,
            dp_count,
            shard_count,
            text_dev,
        )
        holds = jnp.where(dealt_ref[...] == texts, 1.0, 0.0).astype(jnp.bfloat16)
        natural = lax.broadcasted_iota(jnp.int32, (compact, compact), 0)
        moves = jnp.where(natural == slots, 1.0, 0.0).astype(jnp.bfloat16)
        pick_ref[...] = jnp.dot(holds, moves, preferred_element_type=jnp.float32).astype(
            jnp.bfloat16
        )

    query = encode_text(
        step,
        lengths_ref[dealing_ref[me * text_dev + step]],
        hidden_ref,
        (qkv_weight, out_weight, [load.wait for load in loads[:3]], loads[3].wait),
        qkv_bias_ref,
        out_bias_ref,
        gain_ref,
        shift_ref,
        (qkv_ref, context_ref),
    )
    for piece in range(pieces):
        fold_ref[piece : piece + 1, :] = query[:, piece * LANES : (piece + 1) * LANES]
    queries[my_shard, my_dp, step] = fold_ref[...].astype(jnp.bfloat16)

    @pl.when(step == 0)
    def _():
        pl.semaphore_wait(barrier, dp_count + shard_count - 2)
        dp_start(2)

    @pl.when(step == 1)
    def _():
        dp_finish(2)
        shard_start(2)

    @pl.when(step == tail - 1)
    def _():
        dp_start(0)

    @pl.when(step == tail)
    def _():
        dp_finish(0)
        shard_start(0)

    @pl.when(step == text_dev - 1)
    def _():
        dp_start(1)
        shard_finish(2)
        shard_finish(0)
        loads[4].wait()
        dp_finish(1)
        shard_start(1)
        shard_finish(1)

        wide_queries[...] = (
            queries[...].astype(jnp.float32).reshape(compact, pieces, LANES)
        )
        for piece in range(pieces):
            slot_queries[:, piece * LANES : (piece + 1) * LANES] = wide_queries[
                :, piece, :
            ].astype(jnp.bfloat16)
        text_queries[...] = jnp.dot(
            pick_ref[...], slot_queries[...], preferred_element_type=jnp.float32
        ).astype(jnp.bfloat16)

        rows_here = index_rows.shape[0]
        local = cands[...].reshape(padded, LANES) - me * rows_here
        group = local >> 7
        lane = local & (LANES - 1)
        total = jnp.zeros((padded, LANES), jnp.float32)
        rows_step = 1024
        for block in range(rows_here // rows_step):
            scores = lax.dot_general(
                text_queries[...],
                index_rows[block * rows_step : (block + 1) * rows_step, :],
                (((1,), (1,)), ((), ())),
                preferred_element_type=jnp.float32,
            )
            for part in range(rows_step // LANES):
                found = jnp.take_along_axis(
                    scores[:, part * LANES : (part + 1) * LANES],
                    lane,
                    axis=1,
                    mode="promise_in_bounds",
                )
                total = jnp.where(group == block * (rows_step // LANES) + part, found, total)
        terms[...] = total.reshape(terms.shape)

        for off in range(1, shard_count):
            to_shard(terms.at[shard_peer(off)], arrived.at[off], 3, off).start()
        mine = terms[my_shard]
        for off in range(1, shard_count):
            to_shard(terms.at[shard_peer(off)], arrived.at[off], 3, off).wait_recv()
            mine = mine + arrived[off]
        sums[...] = mine
        for off in range(1, dp_count):
            to_dp(sums.at[dp_peer(off)], arrived_dp.at[off], 3, off).start()
        result = sums[my_dp]
        for off in range(1, dp_count):
            to_dp(sums.at[dp_peer(off)], arrived_dp.at[off], 3, off).wait_recv()
            result = result + arrived_dp[off]
        out_ref[...] = result[: out_ref.shape[0], : out_ref.shape[1]]
        for off in range(1, shard_count):
            to_shard(terms.at[shard_peer(off)], arrived.at[off], 3, off).wait_send()
        for off in range(1, dp_count):
            to_dp(sums.at[dp_peer(off)], arrived_dp.at[off], 3, off).wait_send()


def shards(
    hidden,
    lengths,
    dealing,
    candidates,
    index_rows,
    qkv_weight,
    qkv_bias,
    out_weight,
    out_bias,
    norm_gain,
    norm_shift,
):
    text_dev, seq_len, width = hidden.shape
    dp_count, shard_count = lax.axis_size("dp"), lax.axis_size("shard")
    cand_count = candidates.shape[1]
    padded = dp_count * shard_count * SLOTS
    compact = dp_count * shard_count * text_dev
    pieces = width // LANES
    hbm = pl.BlockSpec(memory_space=pl.ANY)

    def whole(*shape):
        return pl.BlockSpec(
            shape, lambda *_: (0,) * len(shape), pipeline_mode=pl.Buffered(1)
        )

    def copy_sems(peers):
        return pltpu.SemaphoreType.DMA((4, peers))

    return pl.pallas_call(
        functools.partial(program_kernel, dp_count, shard_count, text_dev),
        grid_spec=pltpu.PrefetchScalarGridSpec(
            num_scalar_prefetch=2,
            grid=(text_dev,),
            in_specs=[
                pl.BlockSpec((1, seq_len, width), lambda i, *_: (i, 0, 0)),
                whole(1, compact),
                whole(text_dev, cand_count),
                whole(1, 3 * width),
                whole(1, width),
                whole(1, width),
                whole(1, width),
                hbm,
                hbm,
                hbm,
            ],
            out_specs=pl.BlockSpec((text_dev, cand_count), lambda i, *_: (0, 0)),
            scratch_shapes=[
                pltpu.VMEM((width, 3 * width), jnp.bfloat16),
                pltpu.VMEM((width, width), jnp.bfloat16),
                pltpu.VMEM(index_rows.shape, jnp.bfloat16),
                pltpu.VMEM((seq_len, 3 * width), jnp.bfloat16),
                pltpu.VMEM((seq_len, width), jnp.bfloat16),
                pltpu.VMEM((pieces, LANES), jnp.float32),
                pltpu.VMEM((shard_count, dp_count, text_dev, pieces, LANES), jnp.bfloat16),
                pltpu.VMEM((shard_count, dp_count, SLOTS, LANES), jnp.int32),
                pltpu.VMEM((compact, pieces, LANES), jnp.float32),
                pltpu.VMEM((compact, width), jnp.bfloat16),
                pltpu.VMEM((padded, width), jnp.bfloat16),
                pltpu.VMEM((padded, compact), jnp.bfloat16),
                pltpu.VMEM((shard_count, dp_count, SLOTS, LANES), jnp.float32),
                pltpu.VMEM((shard_count, dp_count, SLOTS, LANES), jnp.float32),
                pltpu.VMEM((dp_count, SLOTS, LANES), jnp.float32),
                pltpu.VMEM((dp_count, SLOTS, LANES), jnp.float32),
                pltpu.SemaphoreType.DMA((5,)),
                copy_sems(dp_count),
                copy_sems(dp_count),
                copy_sems(shard_count),
                copy_sems(shard_count),
            ],
        ),
        out_shape=jax.ShapeDtypeStruct((text_dev, cand_count), jnp.float32),
        compiler_params=pltpu.CompilerParams(
            vmem_limit_bytes=56 << 20, collective_id=0, has_side_effects=True
        ),
        name="program",
    )(
        lengths,
        dealing,
        hidden,
        dealing[None, :],
        candidates,
        qkv_bias[None, :],
        out_bias[None, :],
        norm_gain[None, :],
        norm_shift[None, :],
        qkv_weight,
        out_weight,
        index_rows,
    )


def solution(mesh):
    in_specs = (
        P(("dp", "shard"), None, None),
        P(),
        P(),
        P(("dp", "shard"), None),
        P(("dp", "shard"), None),
        P(),
        P(),
        P(),
        P(),
        P(),
        P(),
    )
    out_specs = P(("dp", "shard"), None)
    return jax.shard_map(shards, mesh=mesh, in_specs=in_specs, out_specs=out_specs, check_vma=False)
```

```python
import functools

import jax
import jax.numpy as jnp
from jax import lax
from jax.experimental import pallas as pl
from jax.experimental.pallas import tpu as pltpu
from jax.sharding import PartitionSpec as P

HEADS = 16
HEAD = 64
LANES = 128


SLOTS = 8
BATCH = 2


def encode_text(
    loading, text_len, hidden_ref, weights, bias_ref, out_bias_ref, gain_ref, shift_ref, scratch
):
    qkv_weight, out_weight, qkv_wait, out_wait = weights
    qkv_ref, context_ref = scratch
    seq_len, width = hidden_ref.shape[1], hidden_ref.shape[2]
    states = hidden_ref[0]

    chunk = 512
    for start in range(0, 3 * width, chunk):
        if loading and start % width == 0:
            qkv_wait[start // width]()
        cols = slice(start, start + chunk)
        part = (
            jnp.dot(states, qkv_weight[:, cols], preferred_element_type=jnp.float32)
            + bias_ref[:, cols]
        )
        if start < width:
            part = part * (1.0 / HEAD**0.5)
        qkv_ref[:, cols] = part.astype(jnp.bfloat16)

    lane = lax.broadcasted_iota(jnp.int32, (seq_len, LANES), 1)
    first = lane < HEAD
    key_pos = lax.broadcasted_iota(jnp.int32, (1, seq_len), 1)
    key_bias = jnp.where(key_pos < text_len, 0.0, -1e30).astype(jnp.float32)
    zero = jnp.zeros((seq_len, LANES), jnp.bfloat16)
    ones = jnp.ones((seq_len, LANES), jnp.bfloat16)
    ones_a = jnp.where(first, ones, zero)
    ones_b = jnp.where(first, zero, ones)
    for pair in range(width // LANES):
        base = pair * LANES
        q2 = qkv_ref[:, base : base + LANES]
        k2 = qkv_ref[:, width + base : width + base + LANES]
        v2 = qkv_ref[:, 2 * width + base : 2 * width + base + LANES]
        probs = []
        for keys in (jnp.where(first, k2, zero), jnp.where(first, zero, k2)):
            logits = lax.dot_general(
                q2, keys, (((1,), (1,)), ((), ())), preferred_element_type=jnp.float32
            )
            logits = logits + key_bias
            peak = jnp.max(logits, axis=-1, keepdims=True)
            probs.append(jnp.exp(logits - peak).astype(jnp.bfloat16))
        both = jnp.concatenate(probs, axis=1)
        values = jnp.concatenate(
            [
                jnp.concatenate([jnp.where(first, v2, zero), ones_a], axis=1),
                jnp.concatenate([jnp.where(first, zero, v2), ones_b], axis=1),
            ],
            axis=0,
        )
        mixed = jnp.dot(both, values, preferred_element_type=jnp.float32)
        context_ref[:, base : base + LANES] = (mixed[:, :LANES] / mixed[:, LANES:]).astype(
            jnp.bfloat16
        )

    if loading:
        out_wait()
    resid = (
        states.astype(jnp.float32)
        + jnp.dot(context_ref[...], out_weight[...], preferred_element_type=jnp.float32)
        + out_bias_ref[...]
    )
    centre = jnp.mean(resid, axis=-1, keepdims=True)
    resid = resid - centre
    spread = jnp.mean(resid * resid, axis=-1, keepdims=True)
    row_pos = lax.broadcasted_iota(jnp.int32, (seq_len, 1), 0)
    scale = jnp.where(row_pos < text_len, lax.rsqrt(spread + 1e-05), 0.0)
    total = jnp.sum(resid * scale, axis=0, keepdims=True)
    pooled = total / text_len.astype(jnp.float32) * gain_ref[...] + shift_ref[...]
    return pooled * lax.rsqrt(jnp.sum(pooled * pooled, axis=-1, keepdims=True) + 1e-06)


def slot_order(entries, rows, dp_count, shard_count, text_dev):
    block, row = entries // rows, entries % rows
    place = ((block % dp_count) * shard_count + block // dp_count) * text_dev + row
    return jnp.where(row < text_dev, place, -1)


def program_kernel(
    dp_count,
    shard_count,
    text_dev,
    lengths_ref,
    dealing_ref,
    hidden_ref,
    dealt_ref,
    cand_ref,
    qkv_bias_ref,
    out_bias_ref,
    gain_ref,
    shift_ref,
    qkv_weight_hbm,
    out_weight_hbm,
    index_hbm,
    out_ref,
    qkv_weight,
    out_weight,
    index_rows,
    qkv_ref,
    context_ref,
    fold_ref,
    queries,
    cands,
    wide_queries,
    slot_queries,
    text_queries,
    pick_ref,
    terms,
    arrived,
    load_sems,
    dp_send,
    dp_recv,
    shard_send,
    shard_recv,
    all_send,
    all_recv,
    out_send,
    out_recv,
):
    step = pl.program_id(0)
    my_dp, my_shard = lax.axis_index("dp"), lax.axis_index("shard")
    me = my_dp * shard_count + my_shard
    width = hidden_ref.shape[2]
    pieces = width // LANES
    padded = dp_count * shard_count * SLOTS
    compact = dp_count * shard_count * text_dev

    def dp_peer(off):
        return lax.rem(my_dp + off, dp_count)

    def shard_peer(off):
        return lax.rem(my_shard + off, shard_count)

    def to_dp(src, dst, which, off):
        return pltpu.make_async_remote_copy(
            src_ref=src,
            dst_ref=dst,
            send_sem=dp_send.at[which, off],
            recv_sem=dp_recv.at[which, off],
            device_id=(dp_peer(off), my_shard),
            device_id_type=pl.DeviceIdType.MESH,
        )

    def to_shard(src, dst, which, off):
        return pltpu.make_async_remote_copy(
            src_ref=src,
            dst_ref=dst,
            send_sem=shard_send.at[which, off],
            recv_sem=shard_recv.at[which, off],
            device_id=(my_dp, shard_peer(off)),
            device_id_type=pl.DeviceIdType.MESH,
        )

    tail = max(text_dev - BATCH, 1)
    spans = [pl.ds(0, tail), pl.ds(tail, text_dev - tail)]

    def own(which, dp, shard):
        if which == 2:
            return cands.at[shard, dp]
        return queries.at[shard, dp, spans[which]]

    def column(which, shard):
        if which == 2:
            return cands.at[shard]
        return queries.at[shard, :, spans[which]]

    def dp_start(which):
        for off in range(1, dp_count):
            block = own(which, my_dp, my_shard)
            to_dp(block, block, which, off).start()

    def dp_finish(which):
        for off in range(1, dp_count):
            block = own(which, lax.rem(my_dp + dp_count - off, dp_count), my_shard)
            to_dp(block, block, which, off).wait_recv()

    def sent(which):
        for off in range(1, dp_count):
            block = own(which, my_dp, my_shard)
            to_dp(block, block, which, off).wait_send()
        for off in range(1, shard_count):
            block = column(which, my_shard)
            to_shard(block, block, which, off).wait_send()

    def shard_start(which):
        for off in range(1, shard_count):
            block = column(which, my_shard)
            to_shard(block, block, which, off).start()

    def shard_finish(which):
        for off in range(1, shard_count):
            block = column(which, lax.rem(my_shard + shard_count - off, shard_count))
            to_shard(block, block, which, off).wait_recv()

    others = [(far, off) for far in range(1, dp_count) for off in range(1, shard_count)]
    everyone = others + [(far, 0) for far in range(1, dp_count)]
    everyone += [(0, off) for off in range(1, shard_count)]

    def to_all(src, dst, far, off):
        return pltpu.make_async_remote_copy(
            src_ref=src,
            dst_ref=dst,
            send_sem=all_send.at[far, off],
            recv_sem=all_recv.at[far, off],
            device_id=(dp_peer(far), shard_peer(off)),
            device_id_type=pl.DeviceIdType.MESH,
        )

    def all_start():
        block = own(1, my_dp, my_shard)
        for far, off in everyone:
            to_all(block, block, far, off).start()

    def all_finish():
        for far, off in everyone:
            block = own(
                1,
                lax.rem(my_dp + dp_count - far, dp_count),
                lax.rem(my_shard + shard_count - off, shard_count),
            )
            to_all(block, block, far, off).wait_recv()

    def all_sent():
        block = own(1, my_dp, my_shard)
        for far, off in everyone:
            to_all(block, block, far, off).wait_send()

    loads = [
        pltpu.make_async_copy(
            qkv_weight_hbm.at[:, pl.ds(part * width, width)],
            qkv_weight.at[:, pl.ds(part * width, width)],
            load_sems.at[part],
        )
        for part in range(3)
    ]
    loads.append(pltpu.make_async_copy(out_weight_hbm, out_weight, load_sems.at[3]))
    loads.append(pltpu.make_async_copy(index_hbm, index_rows, load_sems.at[4]))
    barrier = pltpu.get_barrier_semaphore()

    @pl.when(step == 0)
    def _():
        for load in loads[:4]:
            load.start()
        for off in range(1, dp_count):
            pl.semaphore_signal(
                barrier,
                inc=1,
                device_id=(dp_peer(off), my_shard),
                device_id_type=pl.DeviceIdType.MESH,
            )
        for off in range(1, shard_count):
            pl.semaphore_signal(
                barrier,
                inc=1,
                device_id=(my_dp, shard_peer(off)),
                device_id_type=pl.DeviceIdType.MESH,
            )
        for far, off in others:
            pl.semaphore_signal(
                barrier,
                inc=1,
                device_id=(dp_peer(far), shard_peer(off)),
                device_id_type=pl.DeviceIdType.MESH,
            )
        mine = cands.at[my_shard, my_dp]
        mine[...] = jnp.full((SLOTS, LANES), -1, jnp.int32)
        mine[:text_dev, : cand_ref.shape[1]] = cand_ref[...]
        texts = slot_order(
            lax.broadcasted_iota(jnp.int32, (padded, 1), 0), SLOTS, dp_count, shard_count, text_dev
        )
        slots = slot_order(
            lax.broadcasted_iota(jnp.int32, (1, compact), 1),
            text_dev,
            dp_count,
            shard_count,
            text_dev,
        )
        holds = jnp.where(dealt_ref[...] == texts, 1.0, 0.0).astype(jnp.bfloat16)
        natural = lax.broadcasted_iota(jnp.int32, (compact, compact), 0)
        moves = jnp.where(natural == slots, 1.0, 0.0).astype(jnp.bfloat16)
        pick_ref[...] = jnp.dot(holds, moves, preferred_element_type=jnp.float32).astype(
            jnp.bfloat16
        )

    def encode(loading):
        query = encode_text(
            loading,
            lengths_ref[dealing_ref[me * text_dev + step]],
            hidden_ref,
            (qkv_weight, out_weight, [load.wait for load in loads[:3]], loads[3].wait),
            qkv_bias_ref,
            out_bias_ref,
            gain_ref,
            shift_ref,
            (qkv_ref, context_ref),
        )
        for piece in range(pieces):
            fold_ref[piece : piece + 1, :] = query[:, piece * LANES : (piece + 1) * LANES]
        queries[my_shard, my_dp, step] = fold_ref[...].astype(jnp.bfloat16)

    pl.when(step == 0)(functools.partial(encode, True))
    pl.when(step > 0)(functools.partial(encode, False))

    @pl.when(step == 0)
    def _():
        pl.semaphore_wait(barrier, dp_count * shard_count - 1)
        dp_start(2)

    @pl.when(step == 1)
    def _():
        loads[4].start()
        dp_finish(2)
        shard_start(2)

    @pl.when(step == tail - 1)
    def _():
        dp_start(0)

    @pl.when(step == tail)
    def _():
        dp_finish(0)
        shard_start(0)

    @pl.when(step == text_dev - 1)
    def _():
        all_start()
        shard_finish(2)
        shard_finish(0)
        loads[4].wait()
        all_finish()

        wide_queries[...] = (
            queries[...].astype(jnp.float32).reshape(compact, pieces, LANES)
        )
        for piece in range(pieces):
            slot_queries[:, piece * LANES : (piece + 1) * LANES] = wide_queries[
                :, piece, :
            ].astype(jnp.bfloat16)
        text_queries[...] = jnp.dot(
            pick_ref[...], slot_queries[...], preferred_element_type=jnp.float32
        ).astype(jnp.bfloat16)

        rows_here = index_rows.shape[0]
        local = cands[...].reshape(padded, LANES) - me * rows_here
        group = local >> 7
        lane = local & (LANES - 1)
        total = jnp.zeros((padded, LANES), jnp.float32)
        rows_step = 1024
        for block in range(rows_here // rows_step):
            scores = lax.dot_general(
                text_queries[...],
                index_rows[block * rows_step : (block + 1) * rows_step, :],
                (((1,), (1,)), ((), ())),
                preferred_element_type=jnp.float32,
            )
            for part in range(rows_step // LANES):
                found = jnp.take_along_axis(
                    scores[:, part * LANES : (part + 1) * LANES],
                    lane,
                    axis=1,
                    mode="promise_in_bounds",
                )
                total = jnp.where(group == block * (rows_step // LANES) + part, found, total)
        terms[...] = total.reshape(terms.shape)

        def deliver(far, off):
            return pltpu.make_async_remote_copy(
                src_ref=terms.at[shard_peer(off), dp_peer(far)],
                dst_ref=arrived.at[off, far],
                send_sem=out_send.at[far, off],
                recv_sem=out_recv.at[far, off],
                device_id=(dp_peer(far), shard_peer(off)),
                device_id_type=pl.DeviceIdType.MESH,
            )

        for far, off in everyone:
            deliver(far, off).start()
        for which in (0, 2):
            sent(which)
        all_sent()
        result = terms[my_shard, my_dp]
        for far, off in everyone:
            deliver(far, off).wait_recv()
        for far, off in everyone:
            result = result + arrived[off, far]
        out_ref[...] = result[: out_ref.shape[0], : out_ref.shape[1]]
        for far, off in everyone:
            deliver(far, off).wait_send()


def shards(
    hidden,
    lengths,
    dealing,
    candidates,
    index_rows,
    qkv_weight,
    qkv_bias,
    out_weight,
    out_bias,
    norm_gain,
    norm_shift,
):
    text_dev, seq_len, width = hidden.shape
    dp_count, shard_count = lax.axis_size("dp"), lax.axis_size("shard")
    cand_count = candidates.shape[1]
    padded = dp_count * shard_count * SLOTS
    compact = dp_count * shard_count * text_dev
    pieces = width // LANES
    hbm = pl.BlockSpec(memory_space=pl.ANY)

    def whole(*shape):
        return pl.BlockSpec(
            shape, lambda *_: (0,) * len(shape), pipeline_mode=pl.Buffered(1)
        )

    def copy_sems(peers):
        return pltpu.SemaphoreType.DMA((4, peers))

    return pl.pallas_call(
        functools.partial(program_kernel, dp_count, shard_count, text_dev),
        grid_spec=pltpu.PrefetchScalarGridSpec(
            num_scalar_prefetch=2,
            grid=(text_dev,),
            in_specs=[
                pl.BlockSpec((1, seq_len, width), lambda i, *_: (i, 0, 0)),
                whole(1, compact),
                whole(text_dev, cand_count),
                whole(1, 3 * width),
                whole(1, width),
                whole(1, width),
                whole(1, width),
                hbm,
                hbm,
                hbm,
            ],
            out_specs=pl.BlockSpec((text_dev, cand_count), lambda i, *_: (0, 0)),
            scratch_shapes=[
                pltpu.VMEM((width, 3 * width), jnp.bfloat16),
                pltpu.VMEM((width, width), jnp.bfloat16),
                pltpu.VMEM(index_rows.shape, jnp.bfloat16),
                pltpu.VMEM((seq_len, 3 * width), jnp.bfloat16),
                pltpu.VMEM((seq_len, width), jnp.bfloat16),
                pltpu.VMEM((pieces, LANES), jnp.float32),
                pltpu.VMEM((shard_count, dp_count, text_dev, pieces, LANES), jnp.bfloat16),
                pltpu.VMEM((shard_count, dp_count, SLOTS, LANES), jnp.int32),
                pltpu.VMEM((compact, pieces, LANES), jnp.float32),
                pltpu.VMEM((compact, width), jnp.bfloat16),
                pltpu.VMEM((padded, width), jnp.bfloat16),
                pltpu.VMEM((padded, compact), jnp.bfloat16),
                pltpu.VMEM((shard_count, dp_count, SLOTS, LANES), jnp.float32),
                pltpu.VMEM((shard_count, dp_count, SLOTS, LANES), jnp.float32),
                pltpu.SemaphoreType.DMA((5,)),
                copy_sems(dp_count),
                copy_sems(dp_count),
                copy_sems(shard_count),
                copy_sems(shard_count),
                *[pltpu.SemaphoreType.DMA((dp_count, shard_count))] * 4,
            ],
        ),
        out_shape=jax.ShapeDtypeStruct((text_dev, cand_count), jnp.float32),
        compiler_params=pltpu.CompilerParams(
            vmem_limit_bytes=56 << 20, collective_id=0, has_side_effects=True
        ),
        name="program",
    )(
        lengths,
        dealing,
        hidden,
        dealing[None, :],
        candidates,
        qkv_bias[None, :],
        out_bias[None, :],
        norm_gain[None, :],
        norm_shift[None, :],
        qkv_weight,
        out_weight,
        index_rows,
    )


def solution(mesh):
    in_specs = (
        P(("dp", "shard"), None, None),
        P(),
        P(),
        P(("dp", "shard"), None),
        P(("dp", "shard"), None),
        P(),
        P(),
        P(),
        P(),
        P(),
        P(),
    )
    out_specs = P(("dp", "shard"), None)
    return jax.shard_map(shards, mesh=mesh, in_specs=in_specs, out_specs=out_specs, check_vma=False)
```
